128 devices in a mesh: seq: 32 (over z, x, core), tp: 4 (over y).
Axes of the slice: x: 4, y: 4, z: 4, core: 2. Of those that a mesh axis runs over, the one named last changes fastest.
Arguments:
- hidden: bfloat16 [32, 4, 2048], P(None, None, 'seq'), may hold values from -6 to 6
- embedded: bfloat16 [32, 4, 2048], P(None, None, 'seq'), may hold values from -6 to 6
- request_group: int32 [32], replicated, may hold values from 0 to 7, as said below
- group_prompt_length: int32 [8], replicated, may hold values from 1 to 4096, as said below
- prompt_key_cache: bfloat16 [8, 4096, 4096], P(None, 'seq', 'tp'), may hold values from -500 to 500
- prompt_value_cache: bfloat16 [8, 4096, 4096], P(None, 'seq', 'tp'), may hold values from -6 to 6
- input_norm_gain: float32 [2, 2048], P(None, 'seq'), may hold values from 0.25 to 1.75
- query_key_value_weight: bfloat16 [3, 2, 2048, 4096], P(None, None, 'seq', 'tp'), may hold values from -0.09375 to 0.09375
- attention_output_weight: bfloat16 [4096, 2048], P('tp', 'seq'), may hold values from -0.09375 to 0.09375
- middle_norm_gain: float32 [2048], P('seq'), may hold values from 0.25 to 1.75
- gate_up_weight: bfloat16 [2, 2048, 8192], P(None, 'seq', 'tp'), may hold values from -0.125 to 0.125
- adapter_down_weight: bfloat16 [2048, 128], P('seq'), may hold values from -0.125 to 0.125
- adapter_up_weight: bfloat16 [128, 2, 8192], P(None, None, 'tp'), may hold values from -0.5 to 0.5
- down_weight: bfloat16 [8192, 2048], P('tp', 'seq'), may hold values from -0.0625 to 0.0625
- mamba_norm_gain: float32 [2048], P('seq'), may hold values from 0.25 to 1.75
- input_gate_x_weight: bfloat16 [2, 2048, 4096], P(None, 'seq', 'tp'), may hold values from -0.125 to 0.125
- input_step_weight: bfloat16 [2048, 64], P('seq', 'tp'), may hold values from -0.125 to 0.125
- input_bc_weight: bfloat16 [2048, 128], P('seq'), may hold values from -0.125 to 0.125
- convolution_x_taps: float32 [4, 4096], P(None, 'tp'), may hold values from -3 to 3
- convolution_bc_taps: float32 [4, 128], replicated, may hold values from -3 to 3
- prompt_tail_x: bfloat16 [32, 3, 4096], P('seq', None, 'tp'), may hold values from -6 to 6
- prompt_tail_bc: bfloat16 [32, 3, 128], P('seq'), may hold values from -6 to 6
- step_bias: float32 [64], P('tp'), may hold values from -3 to -0.5
- head_decay_rate: float32 [64], P('tp'), may hold values from 0.05 to 2
- head_skip_gain: float32 [64], P('tp'), may hold values from 0.5 to 2
- prompt_state: float32 [32, 64, 64, 64], P('seq', 'tp'), may hold values from -6 to 6
- gated_norm_gain: float32 [4096], P('tp'), may hold values from 0.25 to 1.75
- mamba_output_weight: bfloat16 [4096, 2048], P('tp', 'seq'), may hold values from -0.09375 to 0.09375
Outputs:
- layer_out: bfloat16 [32, 4, 2048], P(None, None, 'seq')
- updated_state: float32 [32, 64, 64, 64], P('seq', 'tp')
The draws below stay inside these ranges and needn't reach their ends.
Inputs may be any that keep to these rules, and one draw needn't show every extreme that they name: `request_group`: every one of the 8 groups serves at least one request. `group_prompt_length`: some group's prompt fills all 4096 positions.
All inputs are finite; a program needn't handle non-finite values.
Results may differ from the reference program's by a relative error of at most 0.012.
The reference program's roundings to bfloat16 on the way count: a program that leaves them out, or rounds other values in their place, can miss the bound.
Values may be sent and summed in bfloat16 or wider, within the bound.
No kernel may reach another device: no remote copies, remote signals or barrier semaphores. Data moves between devices by JAX's collectives and lax.ppermute only.
A program may use at most 128 MiB of HBM per device.

```python
import math
import jax
import jax.numpy as jnp
from jax import lax

MODEL_WIDTH = 2048
HEADS = 32
HD = 128
FEEDFORWARD_UNITS = 8192
ADAPTER_RANK = 128
INNER = 4096
MAMBA_STATE_SIZE = 64
MAMBA_HEAD_SIZE = 64
CONV = 4
NEW = 4
MAMBA_HEADS = 64
REQUEST_COUNT = 32
G = 8
LMAX = 4096
ROWS = 128


def draw_request_group(key, part):
    first, second, third, fourth, fifth = jax.random.split(jax.random.fold_in(key, 11), 5)
    spare = jax.random.randint(first, (REQUEST_COUNT,), 0, G)
    dominant = jax.random.randint(third, (), 0, G)
    share = jax.random.uniform(fourth, (), minval=0.0, maxval=0.7)
    pick = jax.random.uniform(fifth, (REQUEST_COUNT,)) < share
    spare = jnp.where(pick, dominant, spare)
    base = jnp.where(jnp.arange(REQUEST_COUNT) < G, jnp.arange(REQUEST_COUNT), spare)
    order = jax.random.permutation(second, REQUEST_COUNT)
    return base[order].astype(jnp.int32)


def draw_group_prompt_length(key, part):
    first, second = jax.random.split(jax.random.fold_in(key, 23))
    lengths = jax.random.randint(first, (G,), 1, LMAX + 1)
    which = jax.random.randint(second, (), 0, G)
    return jnp.where(jnp.arange(G) == which, LMAX, lengths).astype(jnp.int32)


def draw_prompt_key_cache(key, part):
    first = jax.random.fold_in(jax.random.fold_in(key, 37), 0)
    base = jnp.clip(jax.random.normal(first, (G, LMAX, HEADS * HD), jnp.float32), -6.0, 6.0)
    return base.astype(jnp.bfloat16)


def level_of(rng, shape, cuts, low, top_value):
    loudness, own = 1.0, jax.random.fold_in(rng, 6)
    for position, parts in cuts:
        draws = jnp.exp(jax.random.uniform(jax.random.fold_in(own, position), (parts,), jnp.float32, low / len(cuts), top_value / len(cuts)))
        loudness = loudness * jnp.repeat(draws, shape[position] // parts).reshape([-1 if axis == position else 1 for axis in range(len(shape))])
    return loudness


def gaussian(rng, extent, scale, bound, cuts=(), kind=jnp.bfloat16):
    level = level_of(rng, extent, cuts, -0.22, 0.18) if cuts else 1.0
    drawn = jax.random.normal(rng, extent, jnp.float32) * scale * level
    return jnp.minimum(jnp.maximum(drawn, -bound), bound).astype(kind)


def setup_inputs(seed: int = 0) -> dict:
    splits = jax.random.split(jax.random.key(seed), 29)
    hidden = gaussian(splits[0], (REQUEST_COUNT, NEW, MODEL_WIDTH), 1.0, 6.0, ((2, 32),))
    embedded = gaussian(splits[1], (REQUEST_COUNT, NEW, MODEL_WIDTH), 1.0, 6.0, ((2, 32),))
    request_group = draw_request_group(jax.random.fold_in(splits[28], 71), 0)
    group_prompt_length = draw_group_prompt_length(jax.random.fold_in(splits[28], 71), 0)
    prompt_key_cache = draw_prompt_key_cache(jax.random.fold_in(splits[28], 71), 0)
    prompt_value_cache = gaussian(splits[5], (G, LMAX, HEADS * HD), 1.0, 6.0, ((1, 32), (2, 4)))
    input_norm_gain = jnp.clip(1.0 + 0.15 * jax.random.normal(splits[6], (2, MODEL_WIDTH), jnp.float32), 0.25, 1.75)
    query_key_value_weight = gaussian(splits[7], (3, 2, MODEL_WIDTH, HEADS * HD), (2 * MODEL_WIDTH) ** -0.5, 0.09375, ((2, 32), (3, 4)))
    attention_output_weight = gaussian(splits[8], (HEADS * HD, MODEL_WIDTH), (HEADS * HD) ** -0.5, 0.09375, ((0, 4), (1, 32)))
    middle_norm_gain = jnp.clip(1.0 + 0.15 * jax.random.normal(splits[9], (MODEL_WIDTH,), jnp.float32), 0.25, 1.75)
    gate_up_weight = gaussian(splits[10], (2, MODEL_WIDTH, FEEDFORWARD_UNITS), MODEL_WIDTH ** -0.5, 0.125, ((1, 32), (2, 4)))
    adapter_down_weight = gaussian(splits[11], (MODEL_WIDTH, ADAPTER_RANK), MODEL_WIDTH ** -0.5, 0.125, ((0, 32),))
    adapter_up_weight = gaussian(splits[12], (ADAPTER_RANK, 2, FEEDFORWARD_UNITS), ADAPTER_RANK ** -0.5, 0.5, ((2, 4),))
    down_weight = gaussian(splits[13], (FEEDFORWARD_UNITS, MODEL_WIDTH), FEEDFORWARD_UNITS ** -0.5, 0.0625, ((0, 4), (1, 32)))
    mamba_norm_gain = jnp.clip(1.0 + 0.15 * jax.random.normal(splits[14], (MODEL_WIDTH,), jnp.float32), 0.25, 1.75)
    input_gate_x_weight = gaussian(splits[15], (2, MODEL_WIDTH, INNER), MODEL_WIDTH ** -0.5, 0.125, ((1, 32), (2, 4)))
    input_step_weight = gaussian(splits[16], (MODEL_WIDTH, MAMBA_HEADS), MODEL_WIDTH ** -0.5, 0.125, ((0, 32), (1, 4)))
    input_bc_weight = gaussian(splits[17], (MODEL_WIDTH, 2 * MAMBA_STATE_SIZE), MODEL_WIDTH ** -0.5, 0.125, ((0, 32),))
    convolution_x_taps = gaussian(splits[18], (CONV, INNER), CONV ** -0.5, 3.0, ((1, 4),), jnp.float32)
    convolution_bc_taps = gaussian(splits[19], (CONV, 2 * MAMBA_STATE_SIZE), CONV ** -0.5, 3.0, (), jnp.float32)
    prompt_tail_x = gaussian(splits[20], (REQUEST_COUNT, CONV - 1, INNER), 1.0, 6.0, ((0, 32), (2, 4)))
    prompt_tail_bc = gaussian(splits[21], (REQUEST_COUNT, CONV - 1, 2 * MAMBA_STATE_SIZE), 1.0, 6.0, ((0, 32),))
    step_bias = jnp.clip(-3.0 + 2.5 * jax.random.uniform(splits[22], (MAMBA_HEADS,), jnp.float32) ** level_of(splits[22], (MAMBA_HEADS,), ((0, 4),), -0.2, 0.2), -3.0, -0.5)
    head_decay_rate = jnp.clip(jnp.exp(math.log(2.0) - 3.6888794 * jax.random.uniform(splits[23], (MAMBA_HEADS,), jnp.float32) ** level_of(splits[23], (MAMBA_HEADS,), ((0, 4),), -0.2, 0.2)), 0.05, 2.0)
    head_skip_gain = jnp.clip(0.5 + 1.5 * jax.random.uniform(splits[24], (MAMBA_HEADS,), jnp.float32) ** level_of(splits[24], (MAMBA_HEADS,), ((0, 4),), -0.2, 0.2), 0.5, 2.0)
    prompt_state = gaussian(splits[25], (REQUEST_COUNT, MAMBA_HEADS, MAMBA_HEAD_SIZE, MAMBA_STATE_SIZE), 1.0, 6.0, ((0, 32), (1, 4)), jnp.float32)
    gated_norm_gain = jnp.clip(1.0 + 0.15 * jax.random.normal(splits[26], (INNER,), jnp.float32), 0.25, 1.75)
    mamba_output_weight = gaussian(splits[27], (INNER, MODEL_WIDTH), INNER ** -0.5, 0.09375, ((0, 4), (1, 32)))
    return {"hidden": hidden, "embedded": embedded, "request_group": request_group, "group_prompt_length": group_prompt_length, "prompt_key_cache": prompt_key_cache, "prompt_value_cache": prompt_value_cache, "input_norm_gain": input_norm_gain, "query_key_value_weight": query_key_value_weight, "attention_output_weight": attention_output_weight, "middle_norm_gain": middle_norm_gain, "gate_up_weight": gate_up_weight, "adapter_down_weight": adapter_down_weight, "adapter_up_weight": adapter_up_weight, "down_weight": down_weight, "mamba_norm_gain": mamba_norm_gain, "input_gate_x_weight": input_gate_x_weight, "input_step_weight": input_step_weight, "input_bc_weight": input_bc_weight, "convolution_x_taps": convolution_x_taps, "convolution_bc_taps": convolution_bc_taps, "prompt_tail_x": prompt_tail_x, "prompt_tail_bc": prompt_tail_bc, "step_bias": step_bias, "head_decay_rate": head_decay_rate, "head_skip_gain": head_skip_gain, "prompt_state": prompt_state, "gated_norm_gain": gated_norm_gain, "mamba_output_weight": mamba_output_weight}


EPS = 1e-05
HIGHEST = lax.Precision.HIGHEST

def rms_factor(values):
    return lax.rsqrt(lax.optimization_barrier(jnp.mean(values * values, axis=-1, keepdims=True)) + EPS)

def causal_conv(history, fresh, taps):
    joined = jnp.concatenate([history.astype(jnp.float32), fresh], axis=1)
    length = fresh.shape[1]
    result = jnp.zeros_like(fresh)
    for tap_index in range(taps.shape[0]):
        result = result + taps[tap_index] * joined[:, tap_index:tap_index + length]
    return jax.nn.silu(result)

def state_space_scan(state, inputs, b_mat, c_mat, step_length, decay_factor, head_skip_gain, head_dim):
    requests, new_tok, channels = inputs.shape
    heads_count = channels // head_dim
    outputs = []
    for token_index in range(new_tok):
        per_head = inputs[:, token_index].reshape(requests, heads_count, head_dim)
        state = decay_factor[:, token_index, :, None, None] * state + step_length[:, token_index, :, None, None] * per_head[..., None] * b_mat[:, token_index, None, None, :]
        output = jnp.einsum('rhps,rs->rhp', state, c_mat[:, token_index], precision=HIGHEST)
        outputs.append((output + head_skip_gain[None, :, None] * per_head).reshape(requests, channels))
    return (state, jnp.stack(outputs, axis=1))

def reference(hidden, embedded, request_group, group_prompt_length, prompt_key_cache, prompt_value_cache, input_norm_gain, query_key_value_weight, attention_output_weight, middle_norm_gain, gate_up_weight, adapter_down_weight, adapter_up_weight, down_weight, mamba_norm_gain, input_gate_x_weight, input_step_weight, input_bc_weight, convolution_x_taps, convolution_bc_taps, prompt_tail_x, prompt_tail_bc, step_bias, head_decay_rate, head_skip_gain, prompt_state, gated_norm_gain, mamba_output_weight):
    attn_width = HEADS * HD
    hidden_rows = hidden.reshape(ROWS, MODEL_WIDTH).astype(jnp.float32)
    embed_rows = embedded.reshape(ROWS, MODEL_WIDTH).astype(jnp.float32)
    joined = jnp.concatenate([hidden_rows, embed_rows], axis=1)
    normed_in = (joined * rms_factor(joined) * input_norm_gain.reshape(2 * MODEL_WIDTH)).astype(jnp.bfloat16)
    query = jnp.dot(normed_in, query_key_value_weight[0].reshape(2 * MODEL_WIDTH, attn_width), preferred_element_type=jnp.float32).astype(jnp.bfloat16)
    new_key = jnp.dot(normed_in, query_key_value_weight[1].reshape(2 * MODEL_WIDTH, attn_width), preferred_element_type=jnp.float32).astype(jnp.bfloat16)
    new_value = jnp.dot(normed_in, query_key_value_weight[2].reshape(2 * MODEL_WIDTH, attn_width), preferred_element_type=jnp.float32).astype(jnp.bfloat16)
    scale = 1.0 / HD ** 0.5
    positions = jnp.arange(LMAX)
    causal = jnp.arange(NEW)[:, None] >= jnp.arange(NEW)[None, :]
    row_lengths = group_prompt_length[request_group]

    def attend(items):
        query_req, key_req, value_req, group_index, length = items
        keys = lax.dynamic_index_in_dim(prompt_key_cache, group_index, 0, keepdims=False).astype(jnp.float32).reshape(LMAX, HEADS, HD)
        values = lax.dynamic_index_in_dim(prompt_value_cache, group_index, 0, keepdims=False).astype(jnp.float32).reshape(LMAX, HEADS, HD)
        query_f = query_req.astype(jnp.float32)
        cache_scores = jnp.einsum('thd,phd->htp', query_f, keys, precision=HIGHEST) * scale
        cache_scores = jnp.where((positions < length)[None, None, :], cache_scores, -jnp.inf)
        self_scores = jnp.einsum('thd,uhd->htu', query_f, key_req.astype(jnp.float32), precision=HIGHEST) * scale
        self_scores = jnp.where(causal[None], self_scores, -jnp.inf)
        scores = jnp.concatenate([cache_scores, self_scores], axis=-1)
        maxima = lax.optimization_barrier(jnp.max(scores, axis=-1, keepdims=True))
        weights = jnp.exp(scores - maxima)
        totals = lax.optimization_barrier(jnp.sum(weights, axis=-1))
        summed = jnp.einsum('htp,phd->thd', weights[..., :LMAX], values, precision=HIGHEST)
        summed = summed + jnp.einsum('htu,uhd->thd', weights[..., LMAX:], value_req.astype(jnp.float32), precision=HIGHEST)
        return summed / jnp.transpose(totals)[:, :, None]
    attended = lax.map(attend, (query.reshape(REQUEST_COUNT, NEW, HEADS, HD), new_key.reshape(REQUEST_COUNT, NEW, HEADS, HD), new_value.reshape(REQUEST_COUNT, NEW, HEADS, HD), request_group, row_lengths))
    attn = attended.reshape(ROWS, attn_width).astype(jnp.bfloat16)
    resid = hidden_rows + jnp.dot(attn, attention_output_weight, preferred_element_type=jnp.float32)
    middle_rows = (resid * rms_factor(resid) * middle_norm_gain).astype(jnp.bfloat16)
    adapter_low_rows = jnp.dot(middle_rows, adapter_down_weight, preferred_element_type=jnp.float32).astype(jnp.bfloat16)
    gate_before = jnp.dot(middle_rows, gate_up_weight[0], preferred_element_type=jnp.float32) + jnp.dot(adapter_low_rows, adapter_up_weight[:, 0], preferred_element_type=jnp.float32)
    up_before = jnp.dot(middle_rows, gate_up_weight[1], preferred_element_type=jnp.float32) + jnp.dot(adapter_low_rows, adapter_up_weight[:, 1], preferred_element_type=jnp.float32)
    activated_rows = (jax.nn.silu(gate_before) * up_before).astype(jnp.bfloat16)
    block_out = resid + jnp.dot(activated_rows, down_weight, preferred_element_type=jnp.float32)
    mamba_in = (block_out * rms_factor(block_out) * mamba_norm_gain).astype(jnp.bfloat16)
    z_part = jnp.dot(mamba_in, input_gate_x_weight[0], preferred_element_type=jnp.float32).reshape(REQUEST_COUNT, NEW, INNER)
    x_part = jnp.dot(mamba_in, input_gate_x_weight[1], preferred_element_type=jnp.float32).reshape(REQUEST_COUNT, NEW, INNER)
    dt_raw = jnp.dot(mamba_in, input_step_weight, preferred_element_type=jnp.float32).reshape(REQUEST_COUNT, NEW, MAMBA_HEADS)
    bc_raw = jnp.dot(mamba_in, input_bc_weight, preferred_element_type=jnp.float32).reshape(REQUEST_COUNT, NEW, 2 * MAMBA_STATE_SIZE)
    convolved_x = causal_conv(prompt_tail_x, x_part, convolution_x_taps)
    convolved_bc = causal_conv(prompt_tail_bc, bc_raw, convolution_bc_taps)
    step_length = jax.nn.softplus(dt_raw + step_bias)
    decay_factor = jnp.exp(-step_length * head_decay_rate)
    updated_state, mamba_output = state_space_scan(prompt_state, convolved_x, convolved_bc[..., :MAMBA_STATE_SIZE], convolved_bc[..., MAMBA_STATE_SIZE:], step_length, decay_factor, head_skip_gain, MAMBA_HEAD_SIZE)
    gated = mamba_output * jax.nn.silu(z_part)
    normed_out = (gated * rms_factor(gated) * gated_norm_gain).astype(jnp.bfloat16)
    layer_out = block_out + jnp.dot(normed_out.reshape(ROWS, INNER), mamba_output_weight, preferred_element_type=jnp.float32)
    return (layer_out.reshape(REQUEST_COUNT, NEW, MODEL_WIDTH).astype(jnp.bfloat16), updated_state)
```

```python
import functools
import math

import jax
import jax.numpy as jnp
from jax import lax
from jax.experimental import pallas as pl
from jax.experimental.pallas import tpu as pltpu
from jax.sharding import PartitionSpec as P


HD = 128
MAMBA_HEAD_SIZE = 64
EPS = 1e-05
HIGHEST = lax.Precision.HIGHEST
NEG_FILL = -1e30
BF16 = jnp.bfloat16
F32 = jnp.float32


def core_swap(values):
    size = lax.axis_size("seq")
    return lax.ppermute(values, "seq", [(i, i ^ 1) for i in range(size)])


def project_kernel(weights_count, stat_lane, *refs):
    rows_ref, gain_ref = refs[:2]
    weight_refs = refs[2 : 2 + 2 * weights_count]
    out_ref = refs[-1]
    part = rows_ref[...]
    scaled = (part * gain_ref[...]).astype(BF16)
    at = 0
    for own_ref, partner_ref in zip(weight_refs[:weights_count], weight_refs[weights_count:]):
        stacked = len(own_ref.shape) == 3
        for which in range(own_ref.shape[0] if stacked else 1):
            own = own_ref[which] if stacked else own_ref[...]
            partner = partner_ref[which] if stacked else partner_ref[...]
            lanes = slice(at, at + own.shape[1])
            product = jnp.dot(
                scaled, jnp.concatenate([own, partner], axis=0), preferred_element_type=F32
            )
            at = lanes.stop
            if at < out_ref.shape[1]:
                out_ref[:, lanes] = product.astype(BF16)
    if at < out_ref.shape[1]:
        product = jnp.zeros((part.shape[0], HD), F32)
    total = jnp.sum(part * part, axis=1, keepdims=True)
    high = total.astype(BF16).astype(F32)
    lane = lax.broadcasted_iota(jnp.int32, product.shape, 1)
    product = jnp.where(lane == stat_lane, high, product)
    product = jnp.where(lane == stat_lane + 1, total - high, product)
    out_ref[:, out_ref.shape[1] - HD :] = product.astype(BF16)


def on_chip(values):
    return pltpu.with_memory_space_constraint(values, pltpu.VMEM)


def project(rows, gain, own_weights, partner_weights, stat_lane=0):
    columns = sum(math.prod(weight.shape) // weight.shape[-2] for weight in own_weights)
    columns = columns if stat_lane else columns + HD
    operands = [rows, gain] + list(own_weights) + list(partner_weights)
    return pl.pallas_call(
        functools.partial(project_kernel, len(own_weights), stat_lane),
        in_specs=[pl.BlockSpec(memory_space=pltpu.VMEM)] * len(operands),
        out_specs=pl.BlockSpec(memory_space=pltpu.VMEM),
        out_shape=pltpu.VMEM((rows.shape[0], columns), BF16),
        name="project",
    )(*[on_chip(operand) for operand in operands])


def entry_kernel(
    hidden_hbm,
    embedded_hbm,
    gain_hbm,
    weight_hbm,
    factor_ref,
    mine_out,
    other_out,
    hidden_mine_out,
    hidden_other_out,
    hidden_ref,
    embedded_ref,
    gain_ref,
    weight_ref,
    row_sem,
    gain_sem,
    weight_sem,
):
    core = lax.rem(lax.axis_index("seq"), 2)
    row_copies = []
    for side, parity in enumerate((core, 1 - core)):
        row_copies.append(
            pltpu.make_async_copy(
                hidden_hbm.at[:, parity], hidden_ref.at[side], row_sem.at[0, side]
            )
        )
        row_copies.append(
            pltpu.make_async_copy(
                embedded_hbm.at[:, parity], embedded_ref.at[side], row_sem.at[1, side]
            )
        )
    gain_copy = pltpu.make_async_copy(gain_hbm, gain_ref, gain_sem)
    count, _, columns = weight_ref.shape
    weight_copies = [
        pltpu.make_async_copy(weight_hbm.at[which], weight_ref.at[which], weight_sem.at[which])
        for which in range(count)
    ]
    for copy in row_copies + [gain_copy] + weight_copies:
        copy.start()
    for copy in row_copies + [gain_copy]:
        copy.wait()
    requests = hidden_ref.shape[1]

    def joined(side):
        return jnp.concatenate(
            [
                jnp.concatenate(
                    [ref[side, request].astype(F32) for request in range(requests)], axis=0
                )
                for ref in (hidden_ref, embedded_ref)
            ],
            axis=1,
        )

    gain = jnp.concatenate([gain_ref[0:1, :], gain_ref[1:2, :]], axis=1)
    parts = [joined(0), joined(1)]
    outs = [mine_out, other_out]
    width = count * columns
    half = parts[0].shape[1] // 2
    hidden_mine_out[...] = parts[0][:, :half]
    hidden_other_out[...] = parts[1][:, :half].astype(BF16)
    scaled = []
    for part, parity in zip(parts, (core, 1 - core)):
        factor = jnp.concatenate(
            [factor_ref[request, parity] for request in range(requests)], axis=0
        )
        scaled.append((part * factor * gain).astype(BF16))
    for which in range(count):
        lanes = slice(which * columns, (which + 1) * columns)
        weight_copies[which].wait()
        for side in (1, 0):
            product = jnp.dot(scaled[side], weight_ref[which], preferred_element_type=F32)
            narrow = product.astype(outs[side].dtype)
            outs[side][:, lanes] = narrow
            if which == 0 and side == 1:
                outs[side][:, width : width + columns] = (
                    product - narrow.astype(F32)
                ).astype(BF16)


def enter(hidden, embedded, gain, weight, factor):
    requests, new_tok, half = hidden.shape
    split = (requests // 2, 2, new_tok, half)
    rows = requests // 2 * new_tok
    count, _, columns = weight.shape
    width = count * columns
    vmem = pl.BlockSpec(memory_space=pltpu.VMEM)
    anywhere = pl.BlockSpec(memory_space=pl.ANY)
    side = (2, requests // 2, new_tok, half)
    return pl.pallas_call(
        entry_kernel,
        in_specs=[anywhere] * 4 + [vmem],
        out_specs=[vmem] * 4,
        out_shape=[
            pltpu.VMEM((rows, width), F32),
            pltpu.VMEM((rows, width + columns), BF16),
            pltpu.VMEM((rows, half), F32),
            pltpu.VMEM((rows, half), BF16),
        ],
        scratch_shapes=[
            pltpu.VMEM(side, BF16),
            pltpu.VMEM(side, BF16),
            pltpu.VMEM(gain.shape, F32),
            pltpu.VMEM(weight.shape, BF16),
            pltpu.SemaphoreType.DMA((2, 2)),
            pltpu.SemaphoreType.DMA,
            pltpu.SemaphoreType.DMA((count,)),
        ],
        name="enter",
    )(
        hidden.reshape(split),
        embedded.reshape(split),
        gain,
        weight,
        on_chip(factor.reshape(split[:3] + (factor.shape[-1],))),
    )


def merge_kernel(query_columns, mine_ref, received_ref, out_ref):
    width = mine_ref.shape[1]
    query = slice(0, query_columns)
    low = slice(width, width + query_columns)
    total = (
        mine_ref[:, query]
        + received_ref[:, query].astype(F32)
        + received_ref[:, low].astype(F32)
    )
    high = total.astype(BF16)
    out_ref[:, query] = high
    out_ref[:, low] = (total - high.astype(F32)).astype(BF16)
    others = slice(query_columns, width)
    out_ref[:, others] = (
        mine_ref[:, others] + received_ref[:, others].astype(F32)
    ).astype(BF16)


def merge(mine, received, query_columns):
    return pl.pallas_call(
        functools.partial(merge_kernel, query_columns),
        in_specs=[pl.BlockSpec(memory_space=pltpu.VMEM)] * 2,
        out_specs=pl.BlockSpec(memory_space=pltpu.VMEM),
        out_shape=pltpu.VMEM(received.shape, BF16),
        name="merge",
    )(on_chip(mine), on_chip(received))


def spread_rows(part, new_tok):
    size = lax.axis_size("seq")
    part = part.reshape(size // 2, new_tok, part.shape[1])
    groups = [list(range(core, size, 2)) for core in range(2)]
    return lax.all_to_all(part, "seq", 0, 0, axis_index_groups=groups, tiled=True)


def summed_rows(spread_ref, lanes):
    total = spread_ref[0, :, lanes].astype(F32)
    for source in range(1, spread_ref.shape[0]):
        total = total + spread_ref[source, :, lanes].astype(F32)
    return total


def norm_factor(spread_ref, width, last):
    addends = summed_rows(spread_ref, slice(last - HD, last))
    return lax.rsqrt((addends[:, 0:1] + addends[:, 1:2]) / width + EPS)


def finish_kernel(query_columns, spread_ref, out_ref):
    end = out_ref.shape[1]
    query = summed_rows(spread_ref, slice(0, query_columns)) + summed_rows(
        spread_ref, slice(end, end + query_columns)
    )
    out_ref[:, :query_columns] = query.astype(BF16)
    rest = slice(query_columns, end)
    out_ref[:, rest] = summed_rows(spread_ref, rest).astype(BF16)


def finish_projection(spread, query_columns):
    _, new_tok, columns = spread.shape
    return pl.pallas_call(
        functools.partial(finish_kernel, query_columns),
        in_specs=[pl.BlockSpec(memory_space=pltpu.VMEM)],
        out_specs=pl.BlockSpec(memory_space=pltpu.VMEM),
        out_shape=pltpu.VMEM((new_tok, columns - query_columns), BF16),
        name="finish_projection",
    )(on_chip(spread))


def activation_kernel(width, spread_ref, adapter_ref, out_ref):
    rank, units = adapter_ref.shape[1:]
    factor = norm_factor(spread_ref, width, spread_ref.shape[2])
    low_rank = summed_rows(spread_ref, slice(2 * units, 2 * units + rank)) * factor
    low_rank = low_rank.astype(BF16)

    def pre(which):
        direct = summed_rows(spread_ref, slice(which * units, (which + 1) * units))
        return direct * factor + jnp.dot(
            low_rank, adapter_ref[which], preferred_element_type=F32
        )

    out_ref[...] = (silu(pre(0)) * pre(1)).astype(BF16)


def activate(spread, adapter, width):
    return pl.pallas_call(
        functools.partial(activation_kernel, width),
        in_specs=[pl.BlockSpec(memory_space=pltpu.VMEM)] * 2,
        out_specs=pl.BlockSpec(memory_space=pltpu.VMEM),
        out_shape=pltpu.VMEM((spread.shape[1], adapter.shape[2]), BF16),
        name="activate",
    )(on_chip(spread), on_chip(adapter))


def gather_rows(block):
    size = lax.axis_size("seq")
    full = jnp.broadcast_to(block[None], (size,) + block.shape)
    return lax.all_to_all(full, "seq", 0, 0, tiled=True)


def gather_core_rows(block):
    size = lax.axis_size("seq")
    new_tok, columns = block.shape
    full = jnp.broadcast_to(block[None], (size // 2,) + block.shape)
    groups = [list(range(core, size, 2)) for core in range(2)]
    rows = lax.all_to_all(full, "seq", 0, 0, axis_index_groups=groups, tiled=True)
    return rows.reshape(size // 2 * new_tok, columns)


TP_STEPS = (2, 1, 3)


def swap_all(arrays):
    swapped = []
    for array in arrays:
        swapped.append(core_swap(array))
    return swapped


def tp_total(values, beside=None):
    size = lax.axis_size("tp")
    narrow = values.astype(BF16)
    parts = []
    for step in TP_STEPS:
        pairs = [(i, (i + step) % size) for i in range(size)]
        parts.append(lax.ppermute(narrow, "tp", pairs))
    parts, beside = lax.optimization_barrier((parts, beside))
    total = values
    for part in parts:
        total = total + part.astype(F32)
    return total, beside


def attention_kernel(
    group_ref, limit_ref, query_ref, key_hbm, value_hbm, out_ref, key_ref, value_ref, key_sem, value_sem
):
    rows, width = query_ref.shape
    groups, cache_len, _ = key_hbm.shape
    heads = width // HD
    pairs = heads // 2

    def key_copy(pair):
        lanes = pl.ds(pair * 2 * HD, 2 * HD)
        return pltpu.make_async_copy(
            key_hbm.at[:, :, lanes], key_ref.at[pair], key_sem.at[pair]
        )

    def value_copy(pair):
        lanes = pl.ds(pair * 2 * HD, 2 * HD)
        return pltpu.make_async_copy(
            value_hbm.at[:, :, lanes], value_ref.at[pair], value_sem.at[pair]
        )

    for pair in range(pairs):
        key_copy(pair).start()
        value_copy(pair).start()
    group_of = jnp.concatenate([group_ref[...], group_ref[...]], axis=0)
    position = lax.broadcasted_iota(jnp.int32, (rows, cache_len), 1)
    seen = jnp.where(position < limit_ref[...], 1, 0)
    valid = jnp.concatenate([seen, seen], axis=0) > 0
    lane = lax.broadcasted_iota(jnp.int32, (rows, HD), 1)
    code = jnp.zeros((rows, HD), F32)
    blank = jnp.zeros((rows, HD), BF16)

    def scores_of(pair):
        at = pair * 2 * HD
        first = jnp.concatenate([query_ref[:, at : at + HD], blank], axis=1)
        second = jnp.concatenate([blank, query_ref[:, at + HD : at + 2 * HD]], axis=1)
        query = jnp.concatenate([first, second], axis=0)
        scores = jnp.full((2 * rows, cache_len), NEG_FILL, F32)
        for group in range(groups):
            group_scores = lax.dot_general(
                query,
                key_ref[pair, group],
                (((1,), (1,)), ((), ())),
                preferred_element_type=F32,
            )
            scores = jnp.where(group_of == group, group_scores, scores)
        return jnp.where(valid, scores * (1.0 / math.sqrt(HD)), NEG_FILL)

    def finish(pair, scores, code):
        top = jnp.max(scores, axis=1, keepdims=True)
        weights = jnp.where(valid, jnp.exp(scores - top), 0.0)
        total = jnp.sum(weights, axis=1, keepdims=True)
        wide = jnp.concatenate(
            [
                jnp.where(group_of == group, weights, 0.0).astype(BF16)
                for group in range(groups)
            ],
            axis=1,
        )
        values = value_ref[pair].reshape(groups * cache_len, 2 * HD)
        summed = jnp.dot(wide, values, preferred_element_type=F32)
        safe = jnp.maximum(total, 1e-30)
        scaled = (summed / safe).astype(BF16)
        lse = jnp.where(total > 0.0, top + jnp.log(safe), NEG_FILL)
        high = lse.astype(BF16).astype(F32)
        mid = (lse - high).astype(BF16).astype(F32)
        low = lse - high - mid
        for here in range(2):
            head = 2 * pair + here
            part = slice(here * rows, (here + 1) * rows)
            out_ref[:, head * HD : (head + 1) * HD] = scaled[
                part, here * HD : (here + 1) * HD
            ]
            code = jnp.where(lane == head, high[part], code)
            code = jnp.where(lane == head + heads, mid[part], code)
            code = jnp.where(lane == head + 2 * heads, low[part], code)
        return code

    before = None
    for pair in range(pairs):
        key_copy(pair).wait()
        if pair:
            value_copy(pair - 1).wait()
        scores = scores_of(pair)
        if pair:
            code = finish(pair - 1, before, code)
        before = scores
    value_copy(pairs - 1).wait()
    code = finish(pairs - 1, before, code)
    out_ref[:, width:] = code.astype(BF16)


def attention_partials(query, key_cache, value_cache, group_of, limit):
    rows, width = query.shape
    groups, cache_len, _ = key_cache.shape
    pairs = width // (2 * HD)
    vmem = pl.BlockSpec(memory_space=pltpu.VMEM)
    anywhere = pl.BlockSpec(memory_space=pl.ANY)
    return pl.pallas_call(
        attention_kernel,
        in_specs=[vmem, vmem, vmem, anywhere, anywhere],
        out_specs=vmem,
        out_shape=pltpu.VMEM((rows, width + HD), BF16),
        scratch_shapes=[
            pltpu.VMEM((pairs, groups, cache_len, 2 * HD), BF16),
            pltpu.VMEM((pairs, groups, cache_len, 2 * HD), BF16),
            pltpu.SemaphoreType.DMA((pairs,)),
            pltpu.SemaphoreType.DMA((pairs,)),
        ],
        name="cache_attention",
    )(on_chip(group_of), on_chip(limit), on_chip(query), key_cache, value_cache)


def combine_kernel(spread_ref, own_ref, out_ref):
    new_tok, width = out_ref.shape
    heads = width // HD
    code = spread_ref[:, :, width:].astype(F32)
    peers = code + pltpu.roll(code, HD - heads, 2) + pltpu.roll(code, HD - 2 * heads, 2)
    own = own_ref[...].astype(F32)
    query, keys, values = own[:, :width], own[:, width : 2 * width], own[:, 2 * width :]
    products = jnp.concatenate(
        [query * keys[source : source + 1] for source in range(new_tok)], axis=0
    )
    head_of = lax.broadcasted_iota(jnp.int32, (width, HD), 0) // HD
    collect = jnp.where(
        head_of == lax.broadcasted_iota(jnp.int32, (width, HD), 1), 1.0, 0.0
    ).astype(F32)
    scores = jnp.dot(
        products, collect, precision=HIGHEST, preferred_element_type=F32
    ) * (1.0 / math.sqrt(HD))
    token = lax.broadcasted_iota(jnp.int32, (new_tok, HD), 0)
    own_scores = [
        jnp.where(token >= source, scores[source * new_tok : (source + 1) * new_tok], NEG_FILL)
        for source in range(new_tok)
    ]
    top = jnp.max(peers, axis=0)
    for source in range(new_tok):
        top = jnp.maximum(top, own_scores[source])
    peer_weight = jnp.exp(peers - top[None])
    own_weight = [jnp.exp(own_score - top) for own_score in own_scores]
    total = jnp.sum(peer_weight, axis=0)
    for weight in own_weight:
        total = total + weight
    scale = 1.0 / total
    peer_weight = peer_weight * scale[None]
    own_weight = [weight * scale for weight in own_weight]
    for head in range(heads):
        lanes = slice(head * HD, (head + 1) * HD)
        summed = jnp.sum(
            peer_weight[:, :, head : head + 1] * spread_ref[:, :, lanes].astype(F32), axis=0
        )
        for source in range(new_tok):
            summed = (
                summed
                + own_weight[source][:, head : head + 1] * values[source : source + 1, lanes]
            )
        out_ref[:, lanes] = summed.astype(BF16)


def combine_partials(spread, own):
    _, new_tok, columns = spread.shape
    return pl.pallas_call(
        combine_kernel,
        in_specs=[pl.BlockSpec(memory_space=pltpu.VMEM)] * 2,
        out_specs=pl.BlockSpec(memory_space=pltpu.VMEM),
        out_shape=pltpu.VMEM((new_tok, columns - HD), BF16),
        name="combine",
    )(on_chip(spread), on_chip(own))


def chip_product_kernel(rows_ref, own_ref, partner_ref, out_ref):
    depth = own_ref.shape[1]
    weight = jnp.concatenate([own_ref[...], partner_ref[...]], axis=0)
    out_ref[...] = lax.dot_general(
        rows_ref[:, :depth],
        weight,
        (((1,), (1,)), ((), ())),
        preferred_element_type=F32,
    )


def chip_product(rows, own_weight, partner_weight):
    columns = 2 * own_weight.shape[1]
    return pl.pallas_call(
        chip_product_kernel,
        in_specs=[pl.BlockSpec(memory_space=pltpu.VMEM)] * 3,
        out_specs=pl.BlockSpec(memory_space=pltpu.VMEM),
        out_shape=pltpu.VMEM((rows.shape[0], columns), F32),
        name="chip_product",
    )(on_chip(rows), on_chip(own_weight.T), on_chip(partner_weight.T))


def silu(values):
    return values / (1.0 + jnp.exp(-values))


def mamba_kernel(
    width,
    spread_ref,
    tail_x_ref,
    tail_bc_ref,
    taps_x_ref,
    taps_bc_ref,
    bias_ref,
    rate_ref,
    skip_ref,
    state_ref,
    gain_ref,
    block_ref,
    update_ref,
    b_ref,
    carried_ref,
):
    sources, new_tok, _ = spread_ref.shape
    inner = tail_x_ref.shape[1]
    heads = bias_ref.shape[1]
    state_dim = state_ref.shape[1]
    bc_width = tail_bc_ref.shape[1]
    taps = taps_x_ref.shape[0]
    own = spread_ref[0].astype(F32)
    for source in range(1, sources):
        own = own + spread_ref[source].astype(F32)
    extra = own[:, 2 * inner + bc_width :]
    stat = extra[:, heads : heads + 1] + extra[:, heads + 1 : heads + 2]
    factor = lax.rsqrt(stat / width + EPS)
    own = own * factor
    dt_raw = own[:, 2 * inner + bc_width :][:, :heads]

    def conv(tail_ref, fresh, taps_ref):
        history = tail_ref[...].astype(F32)
        sequence = [history[t : t + 1] for t in range(taps - 1)]
        sequence = sequence + [fresh[t : t + 1] for t in range(new_tok)]
        mixed = []
        for token in range(new_tok):
            result = taps_ref[0:1, :] * sequence[token]
            for tap in range(1, taps):
                result = result + taps_ref[tap : tap + 1, :] * sequence[token + tap]
            mixed.append(silu(result))
        return mixed

    mixed_x = conv(tail_x_ref, own[:, inner : 2 * inner], taps_x_ref)
    mixed_bc = jnp.concatenate(
        conv(tail_bc_ref, own[:, 2 * inner : 2 * inner + bc_width], taps_bc_ref), axis=0
    )
    b_mat = mixed_bc[:, :state_dim]
    c_mat = pltpu.roll(mixed_bc, bc_width - state_dim, 1)[:, :state_dim]
    shifted = dt_raw + bias_ref[...]
    step = jnp.maximum(shifted, 0.0) + jnp.log1p(jnp.exp(-jnp.abs(shifted)))
    decay = jnp.exp(-step * rate_ref[...])
    steps = [step[t : t + 1] for t in range(new_tok)]
    decays = [decay[t : t + 1] for t in range(new_tok)]
    contract = (((1,), (1,)), ((), ()))
    mixing = lax.dot_general(
        c_mat, b_mat, contract, precision=HIGHEST, preferred_element_type=F32
    )
    from_state = lax.dot_general(
        c_mat, state_ref[...], contract, precision=HIGHEST, preferred_element_type=F32
    )
    carried = [decays[0]]
    for token in range(1, new_tok):
        carried.append(carried[-1] * decays[token])
    table = list(carried)
    place = {}
    last = new_tok - 1
    for source in range(new_tok):
        scaled = steps[source]
        for token in range(source, new_tok):
            if token > source:
                scaled = scaled * decays[token]
            weight = scaled * mixing[token : token + 1, source : source + 1]
            if token == source:
                weight = weight + skip_ref[...]
            place[token, source] = len(table)
            table.append(weight)
        place["update", source] = len(table)
        table.append(scaled)
    while len(table) % 8:
        table.append(jnp.zeros_like(table[0]))
    head_of = lax.broadcasted_iota(jnp.int32, (heads, inner), 1) // MAMBA_HEAD_SIZE
    expand = jnp.where(
        head_of == lax.broadcasted_iota(jnp.int32, (heads, inner), 0), 1.0, 0.0
    ).astype(F32)
    wide = jnp.dot(
        jnp.concatenate(table, axis=0), expand, precision=HIGHEST, preferred_element_type=F32
    )
    z_part = own[:, :inner]
    gain = gain_ref[...]
    lane = lax.broadcasted_iota(jnp.int32, (1, HD), 1)
    blocks, extras = [], []
    for token in range(new_tok):
        output = wide[token : token + 1] * from_state[token : token + 1]
        for source in range(token + 1):
            at = place[token, source]
            output = output + wide[at : at + 1] * mixed_x[source]
        gated = output * silu(z_part[token : token + 1])
        total = jnp.sum(gated * gated, axis=1, keepdims=True)
        high = total.astype(BF16).astype(F32)
        blocks.append(gated * gain)
        extras.append(
            jnp.where(lane == 0, high, jnp.where(lane == 1, total - high, 0.0))
        )
    block_ref[:, :inner] = jnp.concatenate(blocks, axis=0).astype(BF16)
    block_ref[:, inner:] = jnp.concatenate(extras, axis=0).astype(BF16)
    update_ref[...] = jnp.concatenate(
        [
            wide[place["update", source] : place["update", source] + 1] * mixed_x[source]
            for source in range(new_tok)
        ],
        axis=0,
    )
    b_ref[...] = b_mat
    carried_ref[...] = carried[last]


def mamba_step(
    spread, tail_x, tail_bc, taps_x, taps_bc, bias, rate, skip, state, gain, width
):
    new_tok = spread.shape[1]
    inner = tail_x.shape[1]
    heads = bias.shape[1]
    operands = (spread, tail_x, tail_bc, taps_x, taps_bc, bias, rate, skip, state, gain)
    return pl.pallas_call(
        functools.partial(mamba_kernel, width),
        in_specs=[pl.BlockSpec(memory_space=pltpu.VMEM)] * len(operands),
        out_specs=[pl.BlockSpec(memory_space=pltpu.VMEM)] * 4,
        out_shape=[
            pltpu.VMEM((new_tok, inner + HD), BF16),
            pltpu.VMEM((new_tok, inner), F32),
            pltpu.VMEM((new_tok, state.shape[1]), F32),
            pltpu.VMEM((1, heads), F32),
        ],
        name="mamba_step",
    )(*[on_chip(operand) for operand in operands])


def state_kernel(state_ref, update_ref, b_ref, carried_ref, out_ref):
    heads = carried_ref.shape[1]
    added = lax.dot_general(
        update_ref[...],
        b_ref[...],
        (((0,), (0,)), ((), ())),
        precision=HIGHEST,
        preferred_element_type=F32,
    )
    size = state_ref.shape[0] // heads
    for head in range(heads):
        part = slice(head * size, (head + 1) * size)
        out_ref[part] = carried_ref[0:1, head : head + 1] * state_ref[part] + added[part]


def state_update(state, update, b_mat, carried):
    return pl.pallas_call(
        state_kernel,
        in_specs=[pl.BlockSpec(memory_space=pltpu.VMEM)] * 4,
        out_specs=pl.BlockSpec(memory_space=pltpu.VMEM),
        out_shape=jax.ShapeDtypeStruct(state.shape, F32),
        name="state_update",
    )(*[on_chip(operand) for operand in (state, update, b_mat, carried)])


def on_device(
    hidden,
    embedded,
    request_group,
    group_prompt_length,
    prompt_key_cache,
    prompt_value_cache,
    input_norm_gain,
    query_key_value_weight,
    attention_output_weight,
    middle_norm_gain,
    gate_up_weight,
    adapter_down_weight,
    adapter_up_weight,
    down_weight,
    mamba_norm_gain,
    input_gate_x_weight,
    input_step_weight,
    input_bc_weight,
    convolution_x_taps,
    convolution_bc_taps,
    prompt_tail_x,
    prompt_tail_bc,
    step_bias,
    head_decay_rate,
    head_skip_gain,
    prompt_state,
    gated_norm_gain,
    mamba_output_weight,
):
    requests, new_tok, columns = hidden.shape
    rows = requests * new_tok
    seq_size = lax.axis_size("seq")
    width = columns * seq_size
    groups, cache_len, width_local = prompt_key_cache.shape
    row_group = jnp.repeat(request_group, new_tok)
    group_match = row_group[:, None] == jnp.arange(groups)[None, :]
    row_length = jnp.sum(jnp.where(group_match, group_prompt_length[None, :], 0), axis=1)
    start = lax.axis_index("seq") * cache_len
    plane = (rows, HD)
    group_of = jnp.broadcast_to(row_group[:, None], plane)
    limit = jnp.broadcast_to((row_length - start)[:, None], plane)

    stat = jnp.sum(jnp.square(hidden.astype(F32)), axis=-1) + jnp.sum(
        jnp.square(embedded.astype(F32)), axis=-1
    )
    stats = lax.all_to_all(
        jnp.broadcast_to(stat.reshape(1, 1, rows), (seq_size, 1, rows)),
        "seq",
        0,
        0,
        tiled=True,
    )
    early = swap_all(
        (
            gate_up_weight,
            attention_output_weight,
            adapter_down_weight,
            middle_norm_gain,
            mamba_norm_gain,
            down_weight,
        ),
    )
    middle_gain = jnp.concatenate([middle_norm_gain, early[3]])[None]
    mamba_gain = jnp.concatenate([mamba_norm_gain, early[4]])[None]
    stats, group_of, limit, middle_gain, mamba_gain = lax.optimization_barrier(
        (stats, group_of, limit, middle_gain, mamba_gain)
    )
    factor = lax.rsqrt(jnp.sum(stats, axis=(0, 1)) / (2 * width) + EPS)
    qkv_weight = query_key_value_weight.reshape(3, 2 * columns, width_local)
    from_mine, from_other, hidden_mine, hidden_other = enter(
        hidden,
        embedded,
        input_norm_gain,
        qkv_weight,
        jnp.broadcast_to(factor[:, None], (rows, 2 * columns)),
    )
    (
        received,
        hidden_partner,
        gate_up_partner,
        output_partner,
        adapter_down_partner,
        down_partner,
    ) = lax.optimization_barrier(
        (
            core_swap(from_other),
            core_swap(hidden_other),
            early[0],
            early[1],
            early[2],
            early[5],
        )
    )
    hidden_rows = jnp.concatenate([hidden_mine, hidden_partner.astype(F32)], axis=1)
    part, hidden_rows = lax.optimization_barrier(
        (merge(from_mine, received, width_local), hidden_rows)
    )
    spread = spread_rows(part, new_tok)
    own_qkv = finish_projection(spread, width_local)
    query = gather_rows(own_qkv[:, :width_local]).reshape(rows, width_local)
    pieces = attention_partials(query, prompt_key_cache, prompt_value_cache, group_of, limit)
    pieces = pieces.reshape(requests, new_tok, width_local + HD)
    own_attn = combine_partials(
        lax.all_to_all(pieces, "seq", 0, 0, tiled=True), own_qkv
    )
    attn = gather_core_rows(own_attn)
    summed, adapter_up = tp_total(
        chip_product(attn, attention_output_weight, output_partner),
        jnp.transpose(adapter_up_weight, (1, 0, 2)),
    )
    resid = hidden_rows + summed

    spread = spread_rows(
        project(
            resid,
            middle_gain,
            [gate_up_weight, adapter_down_weight],
            [gate_up_partner, adapter_down_partner],
        ),
        new_tok,
    )
    own_act = activate(spread, adapter_up, width)
    act = gather_core_rows(own_act)
    mamba_heads = input_step_weight.shape[1]
    step_pad = ((0, 0), (0, HD - mamba_heads))
    gate_x_partner, bc_partner, step_partner, mamba_output_partner = swap_all(
        (input_gate_x_weight, input_bc_weight, input_step_weight, mamba_output_weight),
    )
    beside = (
        jnp.pad(input_step_weight, step_pad),
        jnp.pad(step_partner, step_pad),
        gate_x_partner,
        bc_partner,
        mamba_output_partner,
    )
    summed, beside = tp_total(chip_product(act, down_weight, down_partner), beside)
    step_weight, step_partner, gate_x_partner, bc_partner, mamba_output_partner = beside
    block_out = resid + summed

    inner_local = input_gate_x_weight.shape[2]
    spread = spread_rows(
        project(
            block_out,
            mamba_gain,
            [input_gate_x_weight, input_bc_weight, step_weight],
            [gate_x_partner, bc_partner, step_partner],
            stat_lane=mamba_heads,
        ),
        new_tok,
    )
    state = prompt_state[0]
    block, update, b_mat, carried = mamba_step(
        spread,
        prompt_tail_x[0],
        prompt_tail_bc[0],
        convolution_x_taps,
        convolution_bc_taps,
        step_bias[None],
        head_decay_rate[None],
        head_skip_gain[None],
        state.reshape(inner_local, state.shape[-1]),
        gated_norm_gain[None],
        width,
    )
    normed = gather_core_rows(block)
    normed, update, b_mat, carried = lax.optimization_barrier(
        (normed, update, b_mat, carried)
    )
    updated_state = state_update(
        state.reshape(inner_local, state.shape[-1]), update, b_mat, carried
    ).reshape(prompt_state.shape)
    product = chip_product(normed, mamba_output_weight, mamba_output_partner)
    stat = (
        normed[:, inner_local : inner_local + 1].astype(F32)
        + normed[:, inner_local + 1 : inner_local + 2].astype(F32)
    )
    high = lax.reduce_precision(stat, 8, 7)
    addends = jnp.concatenate(
        [
            jnp.broadcast_to(high, (stat.shape[0], columns)),
            jnp.broadcast_to(stat - high, (stat.shape[0], columns)),
        ],
        axis=1,
    )
    both, updated_state = tp_total(
        jnp.concatenate([product, addends], axis=1), updated_state
    )
    gated_stat = both[:, 2 * columns : 3 * columns] + both[:, 3 * columns :]
    gated_stat = jnp.concatenate([gated_stat, gated_stat], axis=1)
    inner_width = inner_local * lax.axis_size("tp")
    factor = lax.rsqrt(gated_stat / inner_width + EPS)
    layer_out = (block_out + both[:, : 2 * columns] * factor).astype(BF16)
    mine = layer_out[:, :columns].reshape(requests // 2, new_tok, columns)
    other = core_swap(layer_out[:, columns:]).reshape(mine.shape)
    even_core = lax.axis_index("seq") % 2 == 0
    layer_out = jnp.stack(
        [jnp.where(even_core, mine, other), jnp.where(even_core, other, mine)], axis=1
    )
    return layer_out.reshape(requests, new_tok, columns), updated_state


def solution(mesh):
    in_specs = (
        P(None, None, "seq"),
        P(None, None, "seq"),
        P(),
        P(),
        P(None, "seq", "tp"),
        P(None, "seq", "tp"),
        P(None, "seq"),
        P(None, None, "seq", "tp"),
        P("tp", "seq"),
        P("seq"),
        P(None, "seq", "tp"),
        P("seq", None),
        P(None, None, "tp"),
        P("tp", "seq"),
        P("seq"),
        P(None, "seq", "tp"),
        P("seq", "tp"),
        P("seq", None),
        P(None, "tp"),
        P(),
        P("seq", None, "tp"),
        P("seq", None, None),
        P("tp"),
        P("tp"),
        P("tp"),
        P("seq", "tp", None, None),
        P("tp"),
        P("tp", "seq"),
    )
    out_specs = (P(None, None, "seq"), P("seq", "tp", None, None))
    return jax.shard_map(
        on_device, mesh=mesh, in_specs=in_specs, out_specs=out_specs, check_vma=False
    )
```

```python
import functools
import math

import jax
import jax.numpy as jnp
from jax import lax
from jax.experimental import pallas as pl
from jax.experimental.pallas import tpu as pltpu
from jax.sharding import PartitionSpec as P


HD = 128
MAMBA_HEAD_SIZE = 64
EPS = 1e-05
HIGHEST = lax.Precision.HIGHEST
NEG_FILL = -1e30
BF16 = jnp.bfloat16
F32 = jnp.float32


def core_swap(values):
    size = lax.axis_size("seq")
    return lax.ppermute(values, "seq", [(i, i ^ 1) for i in range(size)])


def project_kernel(weights_count, stat_lane, *refs):
    rows_ref, gain_ref = refs[:2]
    weight_refs = refs[2 : 2 + 2 * weights_count]
    out_ref = refs[-1]
    part = rows_ref[...]
    scaled = (part * gain_ref[...]).astype(BF16)
    at = 0
    for own_ref, partner_ref in zip(weight_refs[:weights_count], weight_refs[weights_count:]):
        stacked = len(own_ref.shape) == 3
        for which in range(own_ref.shape[0] if stacked else 1):
            own = own_ref[which] if stacked else own_ref[...]
            partner = partner_ref[which] if stacked else partner_ref[...]
            lanes = slice(at, at + own.shape[1])
            product = jnp.dot(
                scaled, jnp.concatenate([own, partner], axis=0), preferred_element_type=F32
            )
            at = lanes.stop
            if at < out_ref.shape[1]:
                out_ref[:, lanes] = product.astype(BF16)
    if at < out_ref.shape[1]:
        product = jnp.zeros((part.shape[0], HD), F32)
    total = jnp.sum(part * part, axis=1, keepdims=True)
    high = total.astype(BF16).astype(F32)
    lane = lax.broadcasted_iota(jnp.int32, product.shape, 1)
    product = jnp.where(lane == stat_lane, high, product)
    product = jnp.where(lane == stat_lane + 1, total - high, product)
    out_ref[:, out_ref.shape[1] - HD :] = product.astype(BF16)


def on_chip(values):
    return pltpu.with_memory_space_constraint(values, pltpu.VMEM)


def project(rows, gain, own_weights, partner_weights, stat_lane=0):
    columns = sum(math.prod(weight.shape) // weight.shape[-2] for weight in own_weights)
    columns = columns if stat_lane else columns + HD
    operands = [rows, gain] + list(own_weights) + list(partner_weights)
    return pl.pallas_call(
        functools.partial(project_kernel, len(own_weights), stat_lane),
        in_specs=[pl.BlockSpec(memory_space=pltpu.VMEM)] * len(operands),
        out_specs=pl.BlockSpec(memory_space=pltpu.VMEM),
        out_shape=pltpu.VMEM((rows.shape[0], columns), BF16),
        name="project",
    )(*[on_chip(operand) for operand in operands])


def entry_kernel(
    hidden_hbm,
    embedded_hbm,
    gain_hbm,
    weight_hbm,
    factor_ref,
    mine_out,
    other_out,
    hidden_mine_out,
    hidden_other_out,
    hidden_ref,
    embedded_ref,
    gain_ref,
    weight_ref,
    row_sem,
    gain_sem,
    weight_sem,
):
    core = lax.rem(lax.axis_index("seq"), 2)
    row_copies = []
    for side, parity in enumerate((core, 1 - core)):
        row_copies.append(
            pltpu.make_async_copy(
                hidden_hbm.at[:, parity], hidden_ref.at[side], row_sem.at[0, side]
            )
        )
        row_copies.append(
            pltpu.make_async_copy(
                embedded_hbm.at[:, parity], embedded_ref.at[side], row_sem.at[1, side]
            )
        )
    gain_copy = pltpu.make_async_copy(gain_hbm, gain_ref, gain_sem)
    count, _, columns = weight_ref.shape
    weight_copies = [
        pltpu.make_async_copy(weight_hbm.at[which], weight_ref.at[which], weight_sem.at[which])
        for which in range(count)
    ]
    for copy in row_copies + [gain_copy] + weight_copies:
        copy.start()
    for copy in row_copies + [gain_copy]:
        copy.wait()
    requests = hidden_ref.shape[1]

    def joined(side):
        return jnp.concatenate(
            [
                jnp.concatenate(
                    [ref[side, request].astype(F32) for request in range(requests)], axis=0
                )
                for ref in (hidden_ref, embedded_ref)
            ],
            axis=1,
        )

    gain = jnp.concatenate([gain_ref[0:1, :], gain_ref[1:2, :]], axis=1)
    parts = [joined(0), joined(1)]
    outs = [mine_out, other_out]
    width = count * columns
    half = parts[0].shape[1] // 2
    hidden_mine_out[...] = parts[0][:, :half]
    hidden_other_out[...] = parts[1][:, :half].astype(BF16)
    scaled = []
    for part, parity in zip(parts, (core, 1 - core)):
        factor = jnp.concatenate(
            [factor_ref[request, parity] for request in range(requests)], axis=0
        )
        scaled.append((part * factor * gain).astype(BF16))
    for which in range(count):
        lanes = slice(which * columns, (which + 1) * columns)
        weight_copies[which].wait()
        for side in (1, 0):
            product = jnp.dot(scaled[side], weight_ref[which], preferred_element_type=F32)
            narrow = product.astype(outs[side].dtype)
            outs[side][:, lanes] = narrow
            if which == 0 and side == 1:
                outs[side][:, width : width + columns] = (
                    product - narrow.astype(F32)
                ).astype(BF16)


def enter(hidden, embedded, gain, weight, factor):
    requests, new_tok, half = hidden.shape
    split = (requests // 2, 2, new_tok, half)
    rows = requests // 2 * new_tok
    count, _, columns = weight.shape
    width = count * columns
    vmem = pl.BlockSpec(memory_space=pltpu.VMEM)
    anywhere = pl.BlockSpec(memory_space=pl.ANY)
    side = (2, requests // 2, new_tok, half)
    return pl.pallas_call(
        entry_kernel,
        in_specs=[anywhere] * 4 + [vmem],
        out_specs=[vmem] * 4,
        out_shape=[
            pltpu.VMEM((rows, width), F32),
            pltpu.VMEM((rows, width + columns), BF16),
            pltpu.VMEM((rows, half), F32),
            pltpu.VMEM((rows, half), BF16),
        ],
        scratch_shapes=[
            pltpu.VMEM(side, BF16),
            pltpu.VMEM(side, BF16),
            pltpu.VMEM(gain.shape, F32),
            pltpu.VMEM(weight.shape, BF16),
            pltpu.SemaphoreType.DMA((2, 2)),
            pltpu.SemaphoreType.DMA,
            pltpu.SemaphoreType.DMA((count,)),
        ],
        name="enter",
    )(
        hidden.reshape(split),
        embedded.reshape(split),
        gain,
        weight,
        on_chip(factor.reshape(split[:3] + (factor.shape[-1],))),
    )


def merge_kernel(query_columns, mine_ref, received_ref, out_ref):
    width = mine_ref.shape[1]
    query = slice(0, query_columns)
    low = slice(width, width + query_columns)
    total = (
        mine_ref[:, query]
        + received_ref[:, query].astype(F32)
        + received_ref[:, low].astype(F32)
    )
    high = total.astype(BF16)
    out_ref[:, query] = high
    out_ref[:, low] = (total - high.astype(F32)).astype(BF16)
    others = slice(query_columns, width)
    out_ref[:, others] = (
        mine_ref[:, others] + received_ref[:, others].astype(F32)
    ).astype(BF16)


def merge(mine, received, query_columns):
    return pl.pallas_call(
        functools.partial(merge_kernel, query_columns),
        in_specs=[pl.BlockSpec(memory_space=pltpu.VMEM)] * 2,
        out_specs=pl.BlockSpec(memory_space=pltpu.VMEM),
        out_shape=pltpu.VMEM(received.shape, BF16),
        name="merge",
    )(on_chip(mine), on_chip(received))


def spread_rows(part, new_tok):
    size = lax.axis_size("seq")
    part = part.reshape(size // 2, new_tok, part.shape[1])
    groups = [list(range(core, size, 2)) for core in range(2)]
    return lax.all_to_all(part, "seq", 0, 0, axis_index_groups=groups, tiled=True)


def summed_rows(spread_ref, lanes):
    total = spread_ref[0, :, lanes].astype(F32)
    for source in range(1, spread_ref.shape[0]):
        total = total + spread_ref[source, :, lanes].astype(F32)
    return total


def norm_factor(spread_ref, width, last):
    addends = summed_rows(spread_ref, slice(last - HD, last))
    return lax.rsqrt((addends[:, 0:1] + addends[:, 1:2]) / width + EPS)


def finish_kernel(query_columns, spread_ref, out_ref):
    end = out_ref.shape[1]
    query = summed_rows(spread_ref, slice(0, query_columns)) + summed_rows(
        spread_ref, slice(end, end + query_columns)
    )
    out_ref[:, :query_columns] = query.astype(BF16)
    rest = slice(query_columns, end)
    out_ref[:, rest] = summed_rows(spread_ref, rest).astype(BF16)


def finish_projection(spread, query_columns):
    _, new_tok, columns = spread.shape
    return pl.pallas_call(
        functools.partial(finish_kernel, query_columns),
        in_specs=[pl.BlockSpec(memory_space=pltpu.VMEM)],
        out_specs=pl.BlockSpec(memory_space=pltpu.VMEM),
        out_shape=pltpu.VMEM((new_tok, columns - query_columns), BF16),
        name="finish_projection",
    )(on_chip(spread))


def activation_kernel(width, spread_ref, adapter_ref, out_ref):
    rank, units = adapter_ref.shape[1:]
    factor = norm_factor(spread_ref, width, spread_ref.shape[2])
    low_rank = summed_rows(spread_ref, slice(2 * units, 2 * units + rank)) * factor
    low_rank = low_rank.astype(BF16)

    def pre(which):
        direct = summed_rows(spread_ref, slice(which * units, (which + 1) * units))
        return direct * factor + jnp.dot(
            low_rank, adapter_ref[which], preferred_element_type=F32
        )

    out_ref[...] = (silu(pre(0)) * pre(1)).astype(BF16)


def activate(spread, adapter, width):
    return pl.pallas_call(
        functools.partial(activation_kernel, width),
        in_specs=[pl.BlockSpec(memory_space=pltpu.VMEM)] * 2,
        out_specs=pl.BlockSpec(memory_space=pltpu.VMEM),
        out_shape=pltpu.VMEM((spread.shape[1], adapter.shape[2]), BF16),
        name="activate",
    )(on_chip(spread), on_chip(adapter))


def gather_rows(block):
    size = lax.axis_size("seq")
    full = jnp.broadcast_to(block[None], (size,) + block.shape)
    return lax.all_to_all(full, "seq", 0, 0, tiled=True)


def gather_core_rows(block):
    size = lax.axis_size("seq")
    new_tok, columns = block.shape
    full = jnp.broadcast_to(block[None], (size // 2,) + block.shape)
    groups = [list(range(core, size, 2)) for core in range(2)]
    rows = lax.all_to_all(full, "seq", 0, 0, axis_index_groups=groups, tiled=True)
    return rows.reshape(size // 2 * new_tok, columns)


TP_STEPS = (2, 1, 3)


def swap_all(arrays):
    swapped = []
    for array in arrays:
        swapped.append(core_swap(array))
    return swapped


def tp_total(values, beside=None):
    size = lax.axis_size("tp")
    narrow = values.astype(BF16)
    parts = []
    for step in TP_STEPS:
        pairs = [(i, (i + step) % size) for i in range(size)]
        parts.append(lax.ppermute(narrow, "tp", pairs))
    parts, beside = lax.optimization_barrier((parts, beside))
    total = values
    for part in parts:
        total = total + part.astype(F32)
    return total, beside


def attention_kernel(
    group_ref, limit_ref, query_ref, key_hbm, value_hbm, out_ref, key_ref, value_ref, key_sem, value_sem
):
    rows, width = query_ref.shape
    groups, cache_len, _ = key_hbm.shape
    heads = width // HD
    pairs = heads // 2

    def key_copy(pair):
        lanes = pl.ds(pair * 2 * HD, 2 * HD)
        return pltpu.make_async_copy(
            key_hbm.at[:, :, lanes], key_ref.at[pair], key_sem.at[pair]
        )

    def value_copy(pair):
        lanes = pl.ds(pair * 2 * HD, 2 * HD)
        return pltpu.make_async_copy(
            value_hbm.at[:, :, lanes], value_ref.at[pair], value_sem.at[pair]
        )

    for pair in range(pairs):
        key_copy(pair).start()
        value_copy(pair).start()
    group_of = jnp.concatenate([group_ref[...], group_ref[...]], axis=0)
    position = lax.broadcasted_iota(jnp.int32, (rows, cache_len), 1)
    seen = jnp.where(position < limit_ref[...], 1, 0)
    valid = jnp.concatenate([seen, seen], axis=0) > 0
    lane = lax.broadcasted_iota(jnp.int32, (rows, HD), 1)
    code = jnp.zeros((rows, HD), F32)
    blank = jnp.zeros((rows, HD), BF16)

    def scores_of(pair):
        at = pair * 2 * HD
        first = jnp.concatenate([query_ref[:, at : at + HD], blank], axis=1)
        second = jnp.concatenate([blank, query_ref[:, at + HD : at + 2 * HD]], axis=1)
        query = jnp.concatenate([first, second], axis=0)
        scores = jnp.full((2 * rows, cache_len), NEG_FILL, F32)
        for group in range(groups):
            group_scores = lax.dot_general(
                query,
                key_ref[pair, group],
                (((1,), (1,)), ((), ())),
                preferred_element_type=F32,
            )
            scores = jnp.where(group_of == group, group_scores, scores)
        return jnp.where(valid, scores * (1.0 / math.sqrt(HD)), NEG_FILL)

    def finish(pair, scores, code):
        top = jnp.max(scores, axis=1, keepdims=True)
        weights = jnp.where(valid, jnp.exp(scores - top), 0.0)
        total = jnp.sum(weights, axis=1, keepdims=True)
        wide = jnp.concatenate(
            [
                jnp.where(group_of == group, weights, 0.0).astype(BF16)
                for group in range(groups)
            ],
            axis=1,
        )
        values = value_ref[pair].reshape(groups * cache_len, 2 * HD)
        summed = jnp.dot(wide, values, preferred_element_type=F32)
        safe = jnp.maximum(total, 1e-30)
        scaled = (summed / safe).astype(BF16)
        lse = jnp.where(total > 0.0, top + jnp.log(safe), NEG_FILL)
        high = lse.astype(BF16).astype(F32)
        mid = (lse - high).astype(BF16).astype(F32)
        low = lse - high - mid
        for here in range(2):
            head = 2 * pair + here
            part = slice(here * rows, (here + 1) * rows)
            out_ref[:, head * HD : (head + 1) * HD] = scaled[
                part, here * HD : (here + 1) * HD
            ]
            code = jnp.where(lane == head, high[part], code)
            code = jnp.where(lane == head + heads, mid[part], code)
            code = jnp.where(lane == head + 2 * heads, low[part], code)
        return code

    before = None
    for pair in range(pairs):
        key_copy(pair).wait()
        if pair:
            value_copy(pair - 1).wait()
        scores = scores_of(pair)
        if pair:
            code = finish(pair - 1, before, code)
        before = scores
    value_copy(pairs - 1).wait()
    code = finish(pairs - 1, before, code)
    out_ref[:, width:] = code.astype(BF16)


def attention_partials(query, key_cache, value_cache, group_of, limit):
    rows, width = query.shape
    groups, cache_len, _ = key_cache.shape
    pairs = width // (2 * HD)
    vmem = pl.BlockSpec(memory_space=pltpu.VMEM)
    anywhere = pl.BlockSpec(memory_space=pl.ANY)
    return pl.pallas_call(
        attention_kernel,
        in_specs=[vmem, vmem, vmem, anywhere, anywhere],
        out_specs=vmem,
        out_shape=pltpu.VMEM((rows, width + HD), BF16),
        scratch_shapes=[
            pltpu.VMEM((pairs, groups, cache_len, 2 * HD), BF16),
            pltpu.VMEM((pairs, groups, cache_len, 2 * HD), BF16),
            pltpu.SemaphoreType.DMA((pairs,)),
            pltpu.SemaphoreType.DMA((pairs,)),
        ],
        name="cache_attention",
    )(on_chip(group_of), on_chip(limit), on_chip(query), key_cache, value_cache)


def combine_kernel(spread_ref, own_ref, out_ref):
    new_tok, width = out_ref.shape
    heads = width // HD
    code = spread_ref[:, :, width:].astype(F32)
    peers = code + pltpu.roll(code, HD - heads, 2) + pltpu.roll(code, HD - 2 * heads, 2)
    own = own_ref[...].astype(F32)
    query, keys, values = own[:, :width], own[:, width : 2 * width], own[:, 2 * width :]
    products = jnp.concatenate(
        [query * keys[source : source + 1] for source in range(new_tok)], axis=0
    )
    head_of = lax.broadcasted_iota(jnp.int32, (width, HD), 0) // HD
    collect = jnp.where(
        head_of == lax.broadcasted_iota(jnp.int32, (width, HD), 1), 1.0, 0.0
    ).astype(F32)
    scores = jnp.dot(
        products, collect, precision=HIGHEST, preferred_element_type=F32
    ) * (1.0 / math.sqrt(HD))
    token = lax.broadcasted_iota(jnp.int32, (new_tok, HD), 0)
    own_scores = [
        jnp.where(token >= source, scores[source * new_tok : (source + 1) * new_tok], NEG_FILL)
        for source in range(new_tok)
    ]
    top = jnp.max(peers, axis=0)
    for source in range(new_tok):
        top = jnp.maximum(top, own_scores[source])
    peer_weight = jnp.exp(peers - top[None])
    own_weight = [jnp.exp(own_score - top) for own_score in own_scores]
    total = jnp.sum(peer_weight, axis=0)
    for weight in own_weight:
        total = total + weight
    scale = 1.0 / total
    peer_weight = peer_weight * scale[None]
    own_weight = [weight * scale for weight in own_weight]
    for head in range(heads):
        lanes = slice(head * HD, (head + 1) * HD)
        summed = jnp.sum(
            peer_weight[:, :, head : head + 1] * spread_ref[:, :, lanes].astype(F32), axis=0
        )
        for source in range(new_tok):
            summed = (
                summed
                + own_weight[source][:, head : head + 1] * values[source : source + 1, lanes]
            )
        out_ref[:, lanes] = summed.astype(BF16)


def combine_partials(spread, own):
    _, new_tok, columns = spread.shape
    return pl.pallas_call(
        combine_kernel,
        in_specs=[pl.BlockSpec(memory_space=pltpu.VMEM)] * 2,
        out_specs=pl.BlockSpec(memory_space=pltpu.VMEM),
        out_shape=pltpu.VMEM((new_tok, columns - HD), BF16),
        name="combine",
    )(on_chip(spread), on_chip(own))


def chip_product_kernel(rows_ref, own_ref, partner_ref, out_ref):
    depth = own_ref.shape[1]
    weight = jnp.concatenate([own_ref[...], partner_ref[...]], axis=0)
    out_ref[...] = lax.dot_general(
        rows_ref[:, :depth],
        weight,
        (((1,), (1,)), ((), ())),
        preferred_element_type=F32,
    )


def chip_product(rows, own_weight, partner_weight):
    columns = 2 * own_weight.shape[1]
    return pl.pallas_call(
        chip_product_kernel,
        in_specs=[pl.BlockSpec(memory_space=pltpu.VMEM)] * 3,
        out_specs=pl.BlockSpec(memory_space=pltpu.VMEM),
        out_shape=pltpu.VMEM((rows.shape[0], columns), F32),
        name="chip_product",
    )(on_chip(rows), on_chip(own_weight.T), on_chip(partner_weight.T))


def silu(values):
    return values / (1.0 + jnp.exp(-values))


def mamba_kernel(
    width,
    spread_ref,
    tail_x_ref,
    tail_bc_ref,
    taps_x_ref,
    taps_bc_ref,
    bias_ref,
    rate_ref,
    skip_ref,
    state_ref,
    gain_ref,
    block_ref,
    update_ref,
    b_ref,
    carried_ref,
):
    sources, new_tok, _ = spread_ref.shape
    inner = tail_x_ref.shape[1]
    heads = bias_ref.shape[1]
    state_dim = state_ref.shape[1]
    bc_width = tail_bc_ref.shape[1]
    taps = taps_x_ref.shape[0]
    own = spread_ref[0].astype(F32)
    for source in range(1, sources):
        own = own + spread_ref[source].astype(F32)
    extra = own[:, 2 * inner + bc_width :]
    stat = extra[:, heads : heads + 1] + extra[:, heads + 1 : heads + 2]
    factor = lax.rsqrt(stat / width + EPS)
    own = own * factor
    dt_raw = own[:, 2 * inner + bc_width :][:, :heads]

    def conv(tail_ref, fresh, taps_ref):
        history = tail_ref[...].astype(F32)
        sequence = [history[t : t + 1] for t in range(taps - 1)]
        sequence = sequence + [fresh[t : t + 1] for t in range(new_tok)]
        mixed = []
        for token in range(new_tok):
            result = taps_ref[0:1, :] * sequence[token]
            for tap in range(1, taps):
                result = result + taps_ref[tap : tap + 1, :] * sequence[token + tap]
            mixed.append(silu(result))
        return mixed

    mixed_x = conv(tail_x_ref, own[:, inner : 2 * inner], taps_x_ref)
    mixed_bc = jnp.concatenate(
        conv(tail_bc_ref, own[:, 2 * inner : 2 * inner + bc_width], taps_bc_ref), axis=0
    )
    b_mat = mixed_bc[:, :state_dim]
    c_mat = pltpu.roll(mixed_bc, bc_width - state_dim, 1)[:, :state_dim]
    shifted = dt_raw + bias_ref[...]
    step = jnp.maximum(shifted, 0.0) + jnp.log1p(jnp.exp(-jnp.abs(shifted)))
    decay = jnp.exp(-step * rate_ref[...])
    steps = [step[t : t + 1] for t in range(new_tok)]
    decays = [decay[t : t + 1] for t in range(new_tok)]
    contract = (((1,), (1,)), ((), ()))
    mixing = lax.dot_general(
        c_mat, b_mat, contract, precision=HIGHEST, preferred_element_type=F32
    )
    from_state = lax.dot_general(
        c_mat, state_ref[...], contract, precision=HIGHEST, preferred_element_type=F32
    )
    carried = [decays[0]]
    for token in range(1, new_tok):
        carried.append(carried[-1] * decays[token])
    table = list(carried)
    place = {}
    last = new_tok - 1
    for source in range(new_tok):
        scaled = steps[source]
        for token in range(source, new_tok):
            if token > source:
                scaled = scaled * decays[token]
            weight = scaled * mixing[token : token + 1, source : source + 1]
            if token == source:
                weight = weight + skip_ref[...]
            place[token, source] = len(table)
            table.append(weight)
        place["update", source] = len(table)
        table.append(scaled)
    while len(table) % 8:
        table.append(jnp.zeros_like(table[0]))
    head_of = lax.broadcasted_iota(jnp.int32, (heads, inner), 1) // MAMBA_HEAD_SIZE
    expand = jnp.where(
        head_of == lax.broadcasted_iota(jnp.int32, (heads, inner), 0), 1.0, 0.0
    ).astype(F32)
    wide = jnp.dot(
        jnp.concatenate(table, axis=0), expand, precision=HIGHEST, preferred_element_type=F32
    )
    z_part = own[:, :inner]
    gain = gain_ref[...]
    lane = lax.broadcasted_iota(jnp.int32, (1, HD), 1)
    blocks, extras = [], []
    for token in range(new_tok):
        output = wide[token : token + 1] * from_state[token : token + 1]
        for source in range(token + 1):
            at = place[token, source]
            output = output + wide[at : at + 1] * mixed_x[source]
        gated = output * silu(z_part[token : token + 1])
        total = jnp.sum(gated * gated, axis=1, keepdims=True)
        high = total.astype(BF16).astype(F32)
        blocks.append(gated * gain)
        extras.append(
            jnp.where(lane == 0, high, jnp.where(lane == 1, total - high, 0.0))
        )
    block_ref[:, :inner] = jnp.concatenate(blocks, axis=0).astype(BF16)
    block_ref[:, inner:] = jnp.concatenate(extras, axis=0).astype(BF16)
    update_ref[...] = jnp.concatenate(
        [
            wide[place["update", source] : place["update", source] + 1] * mixed_x[source]
            for source in range(new_tok)
        ],
        axis=0,
    )
    b_ref[...] = b_mat
    carried_ref[...] = carried[last]


def mamba_step(
    spread, tail_x, tail_bc, taps_x, taps_bc, bias, rate, skip, state, gain, width
):
    new_tok = spread.shape[1]
    inner = tail_x.shape[1]
    heads = bias.shape[1]
    operands = (spread, tail_x, tail_bc, taps_x, taps_bc, bias, rate, skip, state, gain)
    return pl.pallas_call(
        functools.partial(mamba_kernel, width),
        in_specs=[pl.BlockSpec(memory_space=pltpu.VMEM)] * len(operands),
        out_specs=[pl.BlockSpec(memory_space=pltpu.VMEM)] * 4,
        out_shape=[
            pltpu.VMEM((new_tok, inner + HD), BF16),
            pltpu.VMEM((new_tok, inner), F32),
            pltpu.VMEM((new_tok, state.shape[1]), F32),
            pltpu.VMEM((1, heads), F32),
        ],
        name="mamba_step",
    )(*[on_chip(operand) for operand in operands])


def state_kernel(state_ref, update_ref, b_ref, carried_ref, out_ref):
    heads = carried_ref.shape[1]
    added = lax.dot_general(
        update_ref[...],
        b_ref[...],
        (((0,), (0,)), ((), ())),
        precision=HIGHEST,
        preferred_element_type=F32,
    )
    size = state_ref.shape[0] // heads
    for head in range(heads):
        part = slice(head * size, (head + 1) * size)
        out_ref[part] = carried_ref[0:1, head : head + 1] * state_ref[part] + added[part]


def state_update(state, update, b_mat, carried):
    return pl.pallas_call(
        state_kernel,
        in_specs=[pl.BlockSpec(memory_space=pltpu.VMEM)] * 4,
        out_specs=pl.BlockSpec(memory_space=pltpu.VMEM),
        out_shape=jax.ShapeDtypeStruct(state.shape, F32),
        name="state_update",
    )(*[on_chip(operand) for operand in (state, update, b_mat, carried)])


def on_device(
    hidden,
    embedded,
    request_group,
    group_prompt_length,
    prompt_key_cache,
    prompt_value_cache,
    input_norm_gain,
    query_key_value_weight,
    attention_output_weight,
    middle_norm_gain,
    gate_up_weight,
    adapter_down_weight,
    adapter_up_weight,
    down_weight,
    mamba_norm_gain,
    input_gate_x_weight,
    input_step_weight,
    input_bc_weight,
    convolution_x_taps,
    convolution_bc_taps,
    prompt_tail_x,
    prompt_tail_bc,
    step_bias,
    head_decay_rate,
    head_skip_gain,
    prompt_state,
    gated_norm_gain,
    mamba_output_weight,
):
    requests, new_tok, columns = hidden.shape
    rows = requests * new_tok
    seq_size = lax.axis_size("seq")
    width = columns * seq_size
    groups, cache_len, width_local = prompt_key_cache.shape
    row_group = jnp.repeat(request_group, new_tok)
    group_match = row_group[:, None] == jnp.arange(groups)[None, :]
    row_length = jnp.sum(jnp.where(group_match, group_prompt_length[None, :], 0), axis=1)
    start = lax.axis_index("seq") * cache_len
    plane = (rows, HD)
    group_of = jnp.broadcast_to(row_group[:, None], plane)
    limit = jnp.broadcast_to((row_length - start)[:, None], plane)

    stat = jnp.sum(jnp.square(hidden.astype(F32)), axis=-1) + jnp.sum(
        jnp.square(embedded.astype(F32)), axis=-1
    )
    stats = lax.all_to_all(
        jnp.broadcast_to(stat.reshape(1, 1, rows), (seq_size, 1, rows)),
        "seq",
        0,
        0,
        tiled=True,
    )
    gate_up_partner, middle_gain_partner, mamba_gain_partner = swap_all(
        (gate_up_weight, middle_norm_gain, mamba_norm_gain)
    )
    middle_gain = jnp.concatenate([middle_norm_gain, middle_gain_partner])[None]
    mamba_gain = jnp.concatenate([mamba_norm_gain, mamba_gain_partner])[None]
    stats, group_of, limit, middle_gain, mamba_gain = lax.optimization_barrier(
        (stats, group_of, limit, middle_gain, mamba_gain)
    )
    factor = lax.rsqrt(jnp.sum(stats, axis=(0, 1)) / (2 * width) + EPS)
    qkv_weight = query_key_value_weight.reshape(3, 2 * columns, width_local)
    from_mine, from_other, hidden_mine, hidden_other = enter(
        hidden,
        embedded,
        input_norm_gain,
        qkv_weight,
        jnp.broadcast_to(factor[:, None], (rows, 2 * columns)),
    )
    received, gate_up_partner = lax.optimization_barrier(
        (core_swap(from_other), gate_up_partner)
    )
    part = merge(from_mine, received, width_local)
    spread = spread_rows(part, new_tok)
    own_qkv = finish_projection(spread, width_local)
    query = gather_rows(own_qkv[:, :width_local]).reshape(rows, width_local)
    query, *to_swap = lax.optimization_barrier(
        (
            query,
            hidden_other,
            attention_output_weight,
        )
    )
    hidden_partner, *partners = swap_all(to_swap)
    hidden_rows = jnp.concatenate([hidden_mine, hidden_partner.astype(F32)], axis=1)
    pieces = attention_partials(query, prompt_key_cache, prompt_value_cache, group_of, limit)
    pieces, hidden_rows, partners = lax.optimization_barrier((pieces, hidden_rows, partners))
    (output_partner,) = partners
    pieces = pieces.reshape(requests, new_tok, width_local + HD)
    own_attn = combine_partials(
        lax.all_to_all(pieces, "seq", 0, 0, tiled=True), own_qkv
    )
    attn = gather_core_rows(own_attn)
    wide = swap_all((down_weight, adapter_down_weight))
    summed, beside = tp_total(
        chip_product(attn, attention_output_weight, output_partner),
        (jnp.transpose(adapter_up_weight, (1, 0, 2)), wide),
    )
    adapter_up, (down_partner, adapter_down_partner) = beside
    resid = hidden_rows + summed

    spread = spread_rows(
        project(
            resid,
            middle_gain,
            [gate_up_weight, adapter_down_weight],
            [gate_up_partner, adapter_down_partner],
        ),
        new_tok,
    )
    own_act = activate(spread, adapter_up, width)
    act = gather_core_rows(own_act)
    mamba_heads = input_step_weight.shape[1]
    step_pad = ((0, 0), (0, HD - mamba_heads))
    gate_x_partner, bc_partner, step_partner, mamba_output_partner = swap_all(
        (input_gate_x_weight, input_bc_weight, input_step_weight, mamba_output_weight),
    )
    beside = (
        jnp.pad(input_step_weight, step_pad),
        jnp.pad(step_partner, step_pad),
        gate_x_partner,
        bc_partner,
        mamba_output_partner,
    )
    summed, beside = tp_total(chip_product(act, down_weight, down_partner), beside)
    step_weight, step_partner, gate_x_partner, bc_partner, mamba_output_partner = beside
    block_out = resid + summed

    inner_local = input_gate_x_weight.shape[2]
    spread = spread_rows(
        project(
            block_out,
            mamba_gain,
            [input_gate_x_weight, input_bc_weight, step_weight],
            [gate_x_partner, bc_partner, step_partner],
            stat_lane=mamba_heads,
        ),
        new_tok,
    )
    state = prompt_state[0]
    block, update, b_mat, carried = mamba_step(
        spread,
        prompt_tail_x[0],
        prompt_tail_bc[0],
        convolution_x_taps,
        convolution_bc_taps,
        step_bias[None],
        head_decay_rate[None],
        head_skip_gain[None],
        state.reshape(inner_local, state.shape[-1]),
        gated_norm_gain[None],
        width,
    )
    normed = gather_core_rows(block)
    normed, update, b_mat, carried = lax.optimization_barrier(
        (normed, update, b_mat, carried)
    )
    updated_state = state_update(
        state.reshape(inner_local, state.shape[-1]), update, b_mat, carried
    ).reshape(prompt_state.shape)
    product = chip_product(normed, mamba_output_weight, mamba_output_partner)
    stat = (
        normed[:, inner_local : inner_local + 1].astype(F32)
        + normed[:, inner_local + 1 : inner_local + 2].astype(F32)
    )
    high = lax.reduce_precision(stat, 8, 7)
    addends = jnp.concatenate(
        [
            jnp.broadcast_to(high, (stat.shape[0], columns)),
            jnp.broadcast_to(stat - high, (stat.shape[0], columns)),
        ],
        axis=1,
    )
    both, updated_state = tp_total(jnp.concatenate([product, addends], axis=1), updated_state)
    gated_stat = both[:, 2 * columns : 3 * columns] + both[:, 3 * columns :]
    gated_stat = jnp.concatenate([gated_stat, gated_stat], axis=1)
    inner_width = inner_local * lax.axis_size("tp")
    factor = lax.rsqrt(gated_stat / inner_width + EPS)
    layer_out = (block_out + both[:, : 2 * columns] * factor).astype(BF16)
    mine = layer_out[:, :columns].reshape(requests // 2, new_tok, columns)
    other = core_swap(layer_out[:, columns:]).reshape(mine.shape)
    even_core = lax.axis_index("seq") % 2 == 0
    layer_out = jnp.stack(
        [jnp.where(even_core, mine, other), jnp.where(even_core, other, mine)], axis=1
    )
    return layer_out.reshape(requests, new_tok, columns), updated_state


def solution(mesh):
    in_specs = (
        P(None, None, "seq"),
        P(None, None, "seq"),
        P(),
        P(),
        P(None, "seq", "tp"),
        P(None, "seq", "tp"),
        P(None, "seq"),
        P(None, None, "seq", "tp"),
        P("tp", "seq"),
        P("seq"),
        P(None, "seq", "tp"),
        P("seq", None),
        P(None, None, "tp"),
        P("tp", "seq"),
        P("seq"),
        P(None, "seq", "tp"),
        P("seq", "tp"),
        P("seq", None),
        P(None, "tp"),
        P(),
        P("seq", None, "tp"),
        P("seq", None, None),
        P("tp"),
        P("tp"),
        P("tp"),
        P("seq", "tp", None, None),
        P("tp"),
        P("tp", "seq"),
    )
    out_specs = (P(None, None, "seq"), P("seq", "tp", None, None))
    return jax.shard_map(
        on_device, mesh=mesh, in_specs=in_specs, out_specs=out_specs, check_vma=False
    )
```
